32 devices in a mesh: grp: 2 (over y), sta: 4 (over z), band: 4 (over x, core), src: 1.
Axes of the slice: x: 2, y: 2, z: 4, core: 2. Of those that a mesh axis runs over, the one named last changes fastest.
Arguments:
- spectra: float32 [1, 192, 1024], P('src', ('grp', 'sta', 'band')), parts along dimension 1, may hold values from -6 to 6
- station_place: int32 [192], P('grp'), parts along dimension 0, may hold values from 0 to 95, each once
- tiles: int32 [32, 2], P(('grp', 'sta', 'band')), parts along dimension 0, may hold values from 0 to 1
- observed: float32 [32, 48, 48, 256], P(('grp', 'sta', 'band')), parts along dimension 0, may hold values from -8 to 8
Outputs:
- adjoint: float32 [1, 192, 1024], P('src', ('grp', 'sta', 'band')), parts along dimension 1
The draws below stay inside these ranges and needn't reach their ends.
There are 2 independent parts, one for each index of `grp`. The reference program is written for one: setup_inputs(seed, part) draws one part's arguments, and reference() takes and returns one part's arrays. A program takes and returns all parts, laid end to end along the dimension named above; each array names one. Nothing has to cross between parts.
Inputs may be any that keep to these rules, and one draw needn't show every extreme that they name: station_place is a permutation; block of station s is station_place[s] // 48.
All inputs are finite; a program needn't handle non-finite values.
Results may differ from the reference program's by a relative error of at most 0.00013.
Values sent between devices are 32-bit elements; how exact they have to be, the bound alone decides.
A program may use at most 64 MiB of HBM per device.

```python
import math
import jax
import jax.numpy as jnp
from jax import lax

TILE = 48
FREQ = 512
LAGS = 256
SRC = 1
STATIONS = 96
BLOCKS = 2
TILES = 16


def touch_ends(array, own_key, smallest, largest):
    longest = array.shape.index(max(array.shape))
    spots = []
    for shift in (0, 1):
        where = [jax.random.randint(jax.random.fold_in(own_key, axis), (), 0, length) for axis, length in enumerate(array.shape)]
        where[longest] = (where[longest] + shift) % array.shape[longest]
        spots.append(tuple(where))
    return array.at[spots[0]].set(smallest).at[spots[1]].set(largest)


def levels(rng, dims, shards, least, high):
    def one(position, parts):
        steps = jax.random.uniform(jax.random.fold_in(jax.random.fold_in(rng, 6), position), (parts,), jnp.float32, least / len(shards), high / len(shards))
        return jnp.repeat(jnp.exp(steps), dims[position] // parts).reshape((-1,) + (1,) * (len(dims) - position - 1))

    gain = one(*shards[0])
    for cut in shards[1:]:
        gain = gain * one(*cut)
    return gain


def noise(stream_key, extent, scale, limit, pieces=(), held_as=jnp.bfloat16):
    drawn = scale * jax.random.normal(stream_key, extent, jnp.float32)
    if pieces:
        drawn = drawn * levels(stream_key, extent, pieces, -0.22, 0.18)
    return jnp.clip(drawn, -limit, limit).astype(held_as)


def setup_inputs(seed: int = 0, part: int = 0) -> dict:
    key_of = jax.random.split(jax.random.key(seed), 5)
    own_keys = jax.random.split(jax.random.fold_in(key_of[4], part), 5)
    spectra = noise(own_keys[0], (SRC, STATIONS, 2 * FREQ), 1.0, 6.0, ((1, 16),), jnp.float32)
    station_place = jax.random.permutation(own_keys[1], STATIONS).astype(jnp.int32)
    tiles = touch_ends(jax.random.randint(own_keys[2], (TILES, 2), 0, BLOCKS), jax.random.fold_in(own_keys[2], 1), 0, BLOCKS - 1).astype(jnp.int32)
    observed = noise(own_keys[3], (TILES, TILE, TILE, LAGS), 2.0, 8.0, ((0, 16),), jnp.float32)
    return {"spectra": spectra, "station_place": station_place, "tiles": tiles, "observed": observed}


cubic_weight = 0.1

def dft_table(freqs, lags):
    fvals = jnp.arange(freqs, dtype=jnp.float32)
    tvals = jnp.arange(lags, dtype=jnp.float32) - lags // 2
    phase = math.pi / freqs * fvals[:, None] * tvals[None, :]
    return jnp.concatenate([jnp.cos(phase), -jnp.sin(phase)], 0) * (1.0 / math.sqrt(freqs))

def cross_spectrum(left, right):
    half = left.shape[-1] // 2
    lre = left[:, :, None, :half]
    lim = left[:, :, None, half:]
    rre = right[:, None, :, :half]
    rim = right[:, None, :, half:]
    real = lax.optimization_barrier(jnp.sum(lre * rre + lim * rim, axis=0))
    imag = lax.optimization_barrier(jnp.sum(lim * rre - lre * rim, axis=0))
    return jnp.concatenate([real, imag], -1)

def adjoint_terms(spectral, left, right):
    half = left.shape[-1] // 2
    are = spectral[:, :, :half]
    aim = spectral[:, :, half:]
    hi = lax.Precision.HIGHEST
    lre, lim = (left[:, :, :half], left[:, :, half:])
    rre, rim = (right[:, :, :half], right[:, :, half:])
    row_re = jnp.einsum('pqf,sqf->spf', are, rre, precision=hi) - jnp.einsum('pqf,sqf->spf', aim, rim, precision=hi)
    row_im = jnp.einsum('pqf,sqf->spf', are, rim, precision=hi) + jnp.einsum('pqf,sqf->spf', aim, rre, precision=hi)
    col_re = jnp.einsum('pqf,spf->sqf', are, lre, precision=hi) + jnp.einsum('pqf,spf->sqf', aim, lim, precision=hi)
    col_im = jnp.einsum('pqf,spf->sqf', are, lim, precision=hi) - jnp.einsum('pqf,spf->sqf', aim, lre, precision=hi)
    rows = jnp.concatenate([row_re, row_im], -1)
    cols = jnp.concatenate([col_re, col_im], -1)
    return jnp.concatenate([rows, cols], 1)

def reference(spectra, station_place, tiles, observed):
    count = station_place.shape[0]
    tile = observed.shape[1]
    lags = observed.shape[3]
    width = spectra.shape[2]
    holder = jnp.zeros((count,), jnp.int32).at[station_place].set(jnp.arange(count, dtype=jnp.int32))
    table = dft_table(width // 2, lags)
    offsets = jnp.arange(tile, dtype=jnp.int32)

    def one_tile(items):
        pair, seen = items
        left = spectra[:, holder[pair[0] * tile + offsets]]
        right = spectra[:, holder[pair[1] * tile + offsets]]
        cross = cross_spectrum(left, right).reshape(tile * tile, width)
        lagged = jnp.dot(cross, table, precision=lax.Precision.HIGHEST, preferred_element_type=jnp.float32)
        misfit = lagged - seen.reshape(tile * tile, lags)
        weighted = misfit + cubic_weight * misfit * misfit * misfit
        spectral = jnp.dot(weighted, table.T, precision=lax.Precision.HIGHEST, preferred_element_type=jnp.float32)
        return adjoint_terms(spectral.reshape(tile, tile, width), left, right)
    terms = lax.map(one_tile, (tiles, observed))
    places = (tiles[:, :, None] * tile + offsets[None, None, :]).reshape(-1)
    targets = holder[places]
    flat = jnp.transpose(terms, (1, 0, 2, 3)).reshape(spectra.shape[0], -1, width)
    total = jnp.zeros(spectra.shape, jnp.float32).at[:, targets].add(flat)
    return total * (1.0 / tile)
```

```python
import functools
import math

import jax
import jax.numpy as jnp
import numpy as np
from jax import lax
from jax.experimental import pallas as pl
from jax.experimental.pallas import tpu as pltpu
from jax.sharding import PartitionSpec as P

cubic_weight = 0.1
LANES = 128
MESH = pl.DeviceIdType.MESH


def dft_table(freqs, lags):
    fvals = jnp.arange(freqs, dtype=jnp.float32)
    tvals = jnp.arange(lags, dtype=jnp.float32) - lags // 2
    phase = math.pi / freqs * fvals[:, None] * tvals[None, :]
    return jnp.concatenate([jnp.cos(phase), -jnp.sin(phase)], 0) * (1.0 / math.sqrt(freqs))


def cross_spectrum(left, right):
    half = left.shape[-1] // 2
    lre = left[:, :, None, :half]
    lim = left[:, :, None, half:]
    rre = right[:, None, :, :half]
    rim = right[:, None, :, half:]
    real = jnp.sum(lre * rre + lim * rim, axis=0)
    imag = jnp.sum(lim * rre - lre * rim, axis=0)
    return jnp.concatenate([real, imag], -1)


def adjoint_terms(spectral, left, right):
    half = left.shape[-1] // 2
    are = spectral[:, :, :half]
    aim = spectral[:, :, half:]
    highest = lax.Precision.HIGHEST
    lre, lim = (left[:, :, :half], left[:, :, half:])
    rre, rim = (right[:, :, :half], right[:, :, half:])
    row_re = jnp.einsum("pqf,sqf->spf", are, rre, precision=highest) - jnp.einsum(
        "pqf,sqf->spf", aim, rim, precision=highest
    )
    row_im = jnp.einsum("pqf,sqf->spf", are, rim, precision=highest) + jnp.einsum(
        "pqf,sqf->spf", aim, rre, precision=highest
    )
    col_re = jnp.einsum("pqf,spf->sqf", are, lre, precision=highest) + jnp.einsum(
        "pqf,spf->sqf", aim, lim, precision=highest
    )
    col_im = jnp.einsum("pqf,spf->sqf", are, lim, precision=highest) - jnp.einsum(
        "pqf,spf->sqf", aim, lre, precision=highest
    )
    rows = jnp.concatenate([row_re, row_im], -1)
    cols = jnp.concatenate([col_re, col_im], -1)
    return jnp.concatenate([rows, cols], 1)


def local(spectra, station_place, tiles, observed):
    tile = observed.shape[1]
    lags = observed.shape[3]
    width = spectra.shape[2]
    slots = tiles.shape[0]
    count = station_place.shape[0]
    table = dft_table(width // 2, lags)
    highest = lax.Precision.HIGHEST
    whole = lax.all_gather(spectra[0], ("sta", "band"), axis=0, tiled=True)
    holder = (
        jnp.zeros((count,), jnp.int32).at[station_place].set(jnp.arange(count, dtype=jnp.int32))
    )
    offsets = jnp.arange(tile, dtype=jnp.int32)
    wanted = (tiles[:, :, None] * tile + offsets[None, None, :]).reshape(-1)
    fetched = jnp.take(whole, holder[wanted], axis=0).reshape(slots, 2, tile, width)
    slot = 0
    cross = cross_spectrum(fetched[slot, 0][None], fetched[slot, 1][None]).reshape(
        tile * tile, width
    )
    partial_lags = [jnp.dot(cross, table, precision=highest, preferred_element_type=jnp.float32)]
    lagged = lax.psum(jnp.stack(partial_lags, 0), "src")
    slot = 0
    misfit = lagged[slot] - observed[slot].reshape(tile * tile, lags)
    weighted = misfit + cubic_weight * misfit * misfit * misfit
    spectral = jnp.dot(weighted, table.T, precision=highest, preferred_element_type=jnp.float32)
    terms = adjoint_terms(
        spectral.reshape(tile, tile, width), fetched[slot, 0][None], fetched[slot, 1][None]
    )
    pieces = terms[0]
    select = (station_place[:, None] == wanted[None, :]).astype(jnp.float32)
    mine = lax.psum_scatter(
        jnp.dot(select, pieces, precision=highest, preferred_element_type=jnp.float32),
        ("sta", "band"),
        scatter_dimension=0,
        tiled=True,
    )
    return (mine * (1.0 / tile))[None]

def tables(freqs, lags, lanes):
    fvals = np.arange(freqs, dtype=np.float64)
    tvals = np.arange(lags, dtype=np.float64) - lags // 2
    phase = math.pi / freqs * fvals[:, None] * tvals[None, :]
    scale = 1.0 / math.sqrt(freqs)
    chunks = freqs // lanes
    table = np.stack([np.cos(phase), -np.sin(phase)], 0) * scale
    table = table.reshape(2, chunks, lanes, lags).transpose(1, 0, 2, 3)
    table = table.reshape(chunks, 2 * lanes, lags).astype(np.float32)
    high = table.astype(jnp.bfloat16)
    low = (table - high.astype(np.float32)).astype(jnp.bfloat16)
    down = np.stack([high, low], 0)
    return down, np.ascontiguousarray(down.transpose(0, 1, 3, 2))


def split(value):
    high = value.astype(jnp.bfloat16)
    return high, (value - high.astype(jnp.float32)).astype(jnp.bfloat16)


def mm(a, b):
    return jnp.dot(a, b, preferred_element_type=jnp.float32)


def fused(mesh_sizes, dims, pair_ref, place_ref, spectra_hbm, observed_hbm, down_hbm, up_hbm, out_ref,
          gath, seen, down, up, lag, whigh, wlow, fetched, acc, sendbuf, halfbuf, sumbuf, recvbuf,
          load_sem, table_sem, g1send, g1recv, g2send, g2recv, s1send, s1recv, s2send, s2recv):
    n_sta, n_band = mesh_sizes
    tile, rows, pad, lanes, chunks, block = dims
    n = n_sta * n_band
    pairs = n // 2
    me = lax.axis_index("sta") * n_band + lax.axis_index("band")
    mine, core = me // 2, lax.rem(me, 2)
    real_rows = pl.ds(0, rows)

    def device(pair, side):
        peer = pair * 2 + side
        return {"sta": peer // n_band, "band": lax.rem(peer, n_band)}

    def other(k):
        return lax.rem(mine + k, pairs)

    own = [
        pltpu.make_async_copy(
            spectra_hbm.at[r, pl.ds(h * chunks, chunks), :],
            gath.at[pl.ds(0, chunks), core, mine, r, pl.ds(h * lanes, lanes)],
            load_sem.at[r, h],
        )
        for r in range(rows) for h in range(2)
    ]
    for load in own:
        load.start()
    loads = [
        pltpu.make_async_copy(down_hbm, down, table_sem.at[0]),
        pltpu.make_async_copy(observed_hbm, seen, table_sem.at[1]),
        pltpu.make_async_copy(up_hbm, up, table_sem.at[2]),
    ]
    for load in loads:
        load.start()

    barrier = pltpu.get_barrier_semaphore()

    @pl.loop(1, pairs)
    def _(k):
        pl.semaphore_signal(barrier, inc=1, device_id=device(other(k), core), device_id_type=MESH)

    pl.semaphore_signal(barrier, inc=1, device_id=device(mine, 1 - core), device_id_type=MESH)
    pl.semaphore_wait(barrier, pairs)

    def remote(src, dst, send, recv, pair, side):
        return pltpu.make_async_remote_copy(
            src_ref=src, dst_ref=dst, send_sem=send, recv_sem=recv,
            device_id=device(pair, side), device_id_type=MESH,
        )

    def spread(c, k, holder):
        part = gath.at[c, core, holder, real_rows, :]
        return remote(part, part, g1send.at[c, k], g1recv.at[c, k], other(k), core)

    def forward(c, side):
        part = gath.at[c, side, :, real_rows, :]
        return remote(part, part, g2send.at[c], g2recv.at[c], mine, 1 - core)

    def relay(c):
        @pl.loop(1, pairs)
        def _(k):
            spread(c, k, lax.rem(mine + pairs - k, pairs)).wait_recv()

        forward(c, core).start()

    for load in own:
        load.wait()
    for c in range(chunks):
        @pl.loop(1, pairs)
        def _(k):
            spread(c, k, mine).start()

    count = n * rows
    f32 = jnp.float32
    s_idx = lax.broadcasted_iota(jnp.int32, (count, n * pad), 0)
    g_idx = lax.broadcasted_iota(jnp.int32, (count, n * pad), 1)
    holder = s_idx // rows
    s_row = (holder % 2 * pairs + holder // 2) * pad + s_idx % rows
    expand = (s_row == g_idx).astype(f32)
    places = jnp.broadcast_to(place_ref[...].astype(f32) + 1.0, (8, count))
    places = lax.dot(places, expand, precision=lax.Precision.HIGHEST, preferred_element_type=f32)
    places = jnp.broadcast_to(places[0:1, :], (2 * tile, n * pad))
    j_idx = lax.broadcasted_iota(jnp.int32, (2 * tile, n * pad), 0)
    wanted = jnp.where(j_idx < tile, pair_ref[0, 0] * tile + j_idx, pair_ref[0, 1] * tile + j_idx - tile)
    select32 = (jnp.abs(places - 1.0 - wanted.astype(f32)) < 0.5).astype(f32)
    select = select32.astype(jnp.bfloat16)
    back = jnp.transpose(select32).astype(jnp.bfloat16)
    valid = lax.broadcasted_iota(jnp.int32, (n * pad, 2 * lanes), 0) % pad < rows

    relay(0)
    loads[0].wait()
    steps = tile // block
    span = block * tile
    for c in range(chunks):
        if c + 1 < chunks:
            relay(c + 1)
        forward(c, 1 - core).wait_recv()
        whole = jnp.where(valid, gath[c].reshape(n * pad, 2 * lanes), 0.0)
        high, rest = split(whole)
        low = (whole - high.astype(f32) - rest.astype(f32)).astype(jnp.bfloat16)
        fetched[c] = mm(select, high) + mm(select, rest) + mm(select, low)

        @pl.loop(0, steps)
        def _(b):
            p0 = pl.multiple_of(b * block, block)
            at = pl.ds(pl.multiple_of(b * span, span), span)
            left = fetched[c, pl.ds(p0, block), :]
            lre, lim = left[:, None, :lanes], left[:, None, lanes:]
            right = fetched[c, pl.ds(tile, tile), :]
            rre, rim = right[None, :, :lanes], right[None, :, lanes:]
            real = (lre * rre + lim * rim).reshape(span, lanes)
            imag = (lim * rre - lre * rim).reshape(span, lanes)
            high, low = split(jnp.concatenate([real, imag], -1))
            got = mm(high, down[0, c]) + mm(low, down[0, c]) + mm(high, down[1, c])
            if c > 0:
                got = got + lag[at, :]
            if c < chunks - 1:
                lag[at, :] = got
            else:
                misfit = got - seen[at, :]
                weighted = misfit + cubic_weight * misfit * misfit * misfit
                high, low = split(weighted)
                whigh[at, :] = high
                wlow[at, :] = low

        if c == chunks - 2:
            loads[1].wait()
    loads[2].wait()

    def swap(c):
        return remote(
            sendbuf.at[c, 1 - core, :, real_rows, :], halfbuf.at[c, :, real_rows, :],
            s1send.at[c], s1recv.at[c], mine, 1 - core,
        )

    def deliver(c, k):
        return remote(
            sumbuf.at[c, other(k), real_rows, :], recvbuf.at[c, k, real_rows, :],
            s2send.at[c, k], s2recv.at[c, k], other(k), core,
        )

    def combine(c):
        swap(c).wait_recv()
        sumbuf[c] = sendbuf[c, core] + halfbuf[c]

        @pl.loop(1, pairs)
        def _(k):
            deliver(c, k).start()

    for c in range(chunks):
        acc[pl.ds(tile, tile), :] = jnp.zeros((tile, 2 * lanes), f32)

        @pl.loop(0, steps)
        def _(b):
            p0 = pl.multiple_of(b * block, block)
            at = pl.ds(pl.multiple_of(b * span, span), span)
            high, low = whigh[at, :], wlow[at, :]
            got = mm(high, up[0, c]) + mm(low, up[0, c]) + mm(high, up[1, c])
            got = got.reshape(block, tile, 2 * lanes)
            are, aim = got[:, :, :lanes], got[:, :, lanes:]
            left = fetched[c, pl.ds(p0, block), :]
            lre, lim = left[:, None, :lanes], left[:, None, lanes:]
            right = fetched[c, pl.ds(tile, tile), :]
            rre, rim = right[None, :, :lanes], right[None, :, lanes:]
            acc[pl.ds(p0, block), pl.ds(0, lanes)] = jnp.sum(are * rre - aim * rim, 1)
            acc[pl.ds(p0, block), pl.ds(lanes, lanes)] = jnp.sum(are * rim + aim * rre, 1)
            acc[pl.ds(tile, tile), pl.ds(0, lanes)] += jnp.sum(are * lre + aim * lim, 0)
            acc[pl.ds(tile, tile), pl.ds(lanes, lanes)] += jnp.sum(are * lim - aim * lre, 0)

        high, low = split(acc[...])
        sendbuf[c] = (mm(back, high) + mm(back, low)).reshape(2, pairs, pad, 2 * lanes)
        swap(c).start()
        if c > 0:
            combine(c - 1)
    combine(chunks - 1)

    for c in range(chunks):
        @pl.loop(1, pairs)
        def _(k):
            deliver(c, k).wait_recv()

        total = sumbuf[c, mine]
        for k in range(1, pairs):
            total = total + recvbuf[c, k]
        total = total * (1.0 / tile)
        for h in range(2):
            out_ref[:, h * chunks + c, :] = total[:rows, h * lanes:(h + 1) * lanes]

    for c in range(chunks):
        forward(c, core).wait_send()
        swap(c).wait_send()

        @pl.loop(1, pairs)
        def _(k):
            spread(c, k, mine).wait_send()
            deliver(c, k).wait_send()


def one_kernel(mesh, spectra, station_place, tiles, observed):
    n_sta, n_band = mesh.shape["sta"], mesh.shape["band"]
    n = n_sta * n_band
    tile, lags = observed.shape[1], observed.shape[3]
    rows, width = spectra.shape[1], spectra.shape[2]
    lanes = LANES
    half = width // 2
    chunks = half // lanes
    pad = -(-rows // 8) * 8
    block = 8
    down, up = tables(half, lags, lanes)
    f32, bf16 = jnp.float32, jnp.bfloat16
    dma = pltpu.SemaphoreType.DMA
    anywhere = pl.BlockSpec(memory_space=pl.ANY)
    out = pl.pallas_call(
        functools.partial(fused, (n_sta, n_band), (tile, rows, pad, lanes, chunks, block)),
        out_shape=jax.ShapeDtypeStruct((rows, 2 * chunks, lanes), f32),
        in_specs=[
            pl.BlockSpec(memory_space=pltpu.SMEM), pl.BlockSpec(memory_space=pltpu.VMEM),
            anywhere, anywhere, anywhere, anywhere,
        ],
        out_specs=pl.BlockSpec(memory_space=pltpu.VMEM),
        scratch_shapes=[
            pltpu.VMEM((chunks, 2, n // 2, pad, 2 * lanes), f32),
            pltpu.VMEM((tile * tile, lags), f32),
            pltpu.VMEM(down.shape, bf16),
            pltpu.VMEM(up.shape, bf16),
            pltpu.VMEM((tile * tile, lags), f32),
            pltpu.VMEM((tile * tile, lags), bf16),
            pltpu.VMEM((tile * tile, lags), bf16),
            pltpu.VMEM((chunks, 2 * tile, 2 * lanes), f32),
            pltpu.VMEM((2 * tile, 2 * lanes), f32),
            pltpu.VMEM((chunks, 2, n // 2, pad, 2 * lanes), f32),
            pltpu.VMEM((chunks, n // 2, pad, 2 * lanes), f32),
            pltpu.VMEM((chunks, n // 2, pad, 2 * lanes), f32),
            pltpu.VMEM((chunks, n // 2, pad, 2 * lanes), f32),
            dma((rows, 2)), dma((3,)),
            dma((chunks, n // 2)), dma((chunks, n // 2)), dma((chunks,)), dma((chunks,)),
            dma((chunks,)), dma((chunks,)), dma((chunks, n // 2)), dma((chunks, n // 2)),
        ],
        compiler_params=pltpu.CompilerParams(collective_id=0, has_side_effects=True),
        name="adjoint_kernel",
    )(
        tiles, station_place.reshape(1, -1), spectra.reshape(rows, 2 * chunks, lanes),
        observed.reshape(tile * tile, lags), jnp.asarray(down), jnp.asarray(up),
    )
    return out.reshape(1, rows, width)


def solution(mesh):
    placed = (
        P("src", ("grp", "sta", "band"), None),
        P("grp"),
        P(("grp", "sta", "band"), None),
        P(("grp", "sta", "band"), None, None, None),
    )
    def body(spectra, station_place, tiles, observed):
        fits = (
            mesh.shape["src"] == 1 and mesh.shape["band"] % 2 == 0 and spectra.shape[0] == 1 and tiles.shape[0] == 1
            and spectra.shape[2] % (2 * LANES) == 0 and observed.shape[1] % 8 == 0
        )
        if fits:
            return one_kernel(mesh, spectra, station_place, tiles, observed)
        return local(spectra, station_place, tiles, observed)

    return jax.shard_map(
        body,
        mesh=mesh,
        in_specs=placed,
        out_specs=P("src", ("grp", "sta", "band"), None),
        check_vma=False,
    )
```

```python
import functools
import math

import jax
import jax.numpy as jnp
import numpy as np
from jax import lax
from jax.experimental import pallas as pl
from jax.experimental.pallas import tpu as pltpu
from jax.sharding import PartitionSpec as P

cubic_weight = 0.1
LANES = 128
MESH = pl.DeviceIdType.MESH


def dft_table(freqs, lags):
    fvals = jnp.arange(freqs, dtype=jnp.float32)
    tvals = jnp.arange(lags, dtype=jnp.float32) - lags // 2
    phase = math.pi / freqs * fvals[:, None] * tvals[None, :]
    return jnp.concatenate([jnp.cos(phase), -jnp.sin(phase)], 0) * (1.0 / math.sqrt(freqs))


def cross_spectrum(left, right):
    half = left.shape[-1] // 2
    lre = left[:, :, None, :half]
    lim = left[:, :, None, half:]
    rre = right[:, None, :, :half]
    rim = right[:, None, :, half:]
    real = jnp.sum(lre * rre + lim * rim, axis=0)
    imag = jnp.sum(lim * rre - lre * rim, axis=0)
    return jnp.concatenate([real, imag], -1)


def adjoint_terms(spectral, left, right):
    half = left.shape[-1] // 2
    are = spectral[:, :, :half]
    aim = spectral[:, :, half:]
    highest = lax.Precision.HIGHEST
    lre, lim = (left[:, :, :half], left[:, :, half:])
    rre, rim = (right[:, :, :half], right[:, :, half:])
    row_re = jnp.einsum("pqf,sqf->spf", are, rre, precision=highest) - jnp.einsum(
        "pqf,sqf->spf", aim, rim, precision=highest
    )
    row_im = jnp.einsum("pqf,sqf->spf", are, rim, precision=highest) + jnp.einsum(
        "pqf,sqf->spf", aim, rre, precision=highest
    )
    col_re = jnp.einsum("pqf,spf->sqf", are, lre, precision=highest) + jnp.einsum(
        "pqf,spf->sqf", aim, lim, precision=highest
    )
    col_im = jnp.einsum("pqf,spf->sqf", are, lim, precision=highest) - jnp.einsum(
        "pqf,spf->sqf", aim, lre, precision=highest
    )
    rows = jnp.concatenate([row_re, row_im], -1)
    cols = jnp.concatenate([col_re, col_im], -1)
    return jnp.concatenate([rows, cols], 1)


def local(spectra, station_place, tiles, observed):
    tile = observed.shape[1]
    lags = observed.shape[3]
    width = spectra.shape[2]
    slots = tiles.shape[0]
    count = station_place.shape[0]
    table = dft_table(width // 2, lags)
    highest = lax.Precision.HIGHEST
    whole = lax.all_gather(spectra[0], ("sta", "band"), axis=0, tiled=True)
    holder = (
        jnp.zeros((count,), jnp.int32).at[station_place].set(jnp.arange(count, dtype=jnp.int32))
    )
    offsets = jnp.arange(tile, dtype=jnp.int32)
    wanted = (tiles[:, :, None] * tile + offsets[None, None, :]).reshape(-1)
    fetched = jnp.take(whole, holder[wanted], axis=0).reshape(slots, 2, tile, width)
    slot = 0
    cross = cross_spectrum(fetched[slot, 0][None], fetched[slot, 1][None]).reshape(
        tile * tile, width
    )
    partial_lags = [jnp.dot(cross, table, precision=highest, preferred_element_type=jnp.float32)]
    lagged = lax.psum(jnp.stack(partial_lags, 0), "src")
    slot = 0
    misfit = lagged[slot] - observed[slot].reshape(tile * tile, lags)
    weighted = misfit + cubic_weight * misfit * misfit * misfit
    spectral = jnp.dot(weighted, table.T, precision=highest, preferred_element_type=jnp.float32)
    terms = adjoint_terms(
        spectral.reshape(tile, tile, width), fetched[slot, 0][None], fetched[slot, 1][None]
    )
    pieces = terms[0]
    select = (station_place[:, None] == wanted[None, :]).astype(jnp.float32)
    mine = lax.psum_scatter(
        jnp.dot(select, pieces, precision=highest, preferred_element_type=jnp.float32),
        ("sta", "band"),
        scatter_dimension=0,
        tiled=True,
    )
    return (mine * (1.0 / tile))[None]

def tables(freqs, lags, lanes):
    fvals = np.arange(freqs, dtype=np.float64)
    tvals = np.arange(lags, dtype=np.float64) - lags // 2
    phase = math.pi / freqs * fvals[:, None] * tvals[None, :]
    scale = 1.0 / math.sqrt(freqs)
    chunks = freqs // lanes
    table = np.stack([np.cos(phase), -np.sin(phase)], 0) * scale
    table = table.reshape(2, chunks, lanes, lags).transpose(1, 0, 2, 3)
    table = table.reshape(chunks, 2 * lanes, lags).astype(np.float32)
    high = table.astype(jnp.bfloat16)
    low = (table - high.astype(np.float32)).astype(jnp.bfloat16)
    down = np.stack([high, low], 0)
    return down, np.ascontiguousarray(down.transpose(0, 1, 3, 2))


def split(value):
    high = value.astype(jnp.bfloat16)
    return high, (value - high.astype(jnp.float32)).astype(jnp.bfloat16)


def mm(a, b):
    return jnp.dot(a, b, preferred_element_type=jnp.float32)


def fused(mesh_sizes, dims, pair_ref, place_ref, spectra_hbm, observed_hbm, down_hbm, up_hbm, out_ref,
          gath, seen, down, up, lag, whigh, wlow, fetched, acc, sendbuf, halfbuf, sumbuf, recvbuf,
          load_sem, table_sem, g1send, g1recv, g2send, g2recv, s1send, s1recv, s2send, s2recv):
    n_sta, n_band = mesh_sizes
    tile, rows, pad, lanes, chunks, block = dims
    n = n_sta * n_band
    pairs = n // 2
    me = lax.axis_index("sta") * n_band + lax.axis_index("band")
    mine, core = me // 2, lax.rem(me, 2)
    real_rows = pl.ds(0, rows)

    def device(pair, side):
        peer = pair * 2 + side
        return {"sta": peer // n_band, "band": lax.rem(peer, n_band)}

    def other(k):
        return lax.rem(mine + k, pairs)

    own = [
        pltpu.make_async_copy(
            spectra_hbm.at[r, pl.ds(h * chunks, chunks), :],
            gath.at[pl.ds(0, chunks), core, mine, r, pl.ds(h * lanes, lanes)],
            load_sem.at[r, h],
        )
        for r in range(rows) for h in range(2)
    ]
    for load in own:
        load.start()
    loads = [
        pltpu.make_async_copy(down_hbm, down, table_sem.at[0]),
        pltpu.make_async_copy(observed_hbm, seen, table_sem.at[1]),
        pltpu.make_async_copy(up_hbm, up, table_sem.at[2]),
    ]
    for load in loads:
        load.start()

    barrier = pltpu.get_barrier_semaphore()

    @pl.loop(1, pairs)
    def _(k):
        pl.semaphore_signal(barrier, inc=1, device_id=device(other(k), core), device_id_type=MESH)

    pl.semaphore_signal(barrier, inc=1, device_id=device(mine, 1 - core), device_id_type=MESH)
    pl.semaphore_wait(barrier, pairs)

    def remote(src, dst, send, recv, pair, side):
        return pltpu.make_async_remote_copy(
            src_ref=src, dst_ref=dst, send_sem=send, recv_sem=recv,
            device_id=device(pair, side), device_id_type=MESH,
        )

    def spread(c, k, holder):
        part = gath.at[c, core, holder, real_rows, :]
        return remote(part, part, g1send.at[c, k], g1recv.at[c, k], other(k), core)

    def forward(c, side):
        part = gath.at[c, side, :, real_rows, :]
        return remote(part, part, g2send.at[c], g2recv.at[c], mine, 1 - core)

    def relay(c):
        @pl.loop(1, pairs)
        def _(k):
            spread(c, k, lax.rem(mine + pairs - k, pairs)).wait_recv()

        forward(c, core).start()

    for load in own:
        load.wait()
    for c in range(chunks):
        @pl.loop(1, pairs)
        def _(k):
            spread(c, k, mine).start()

    count = n * rows
    f32 = jnp.float32
    s_idx = lax.broadcasted_iota(jnp.int32, (count, n * pad), 0)
    g_idx = lax.broadcasted_iota(jnp.int32, (count, n * pad), 1)
    holder = s_idx // rows
    s_row = (holder % 2 * pairs + holder // 2) * pad + s_idx % rows
    expand = (s_row == g_idx).astype(f32)
    places = jnp.broadcast_to(place_ref[...].astype(f32) + 1.0, (8, count))
    places = lax.dot(places, expand, precision=lax.Precision.HIGHEST, preferred_element_type=f32)
    places = jnp.broadcast_to(places[0:1, :], (2 * tile, n * pad))
    j_idx = lax.broadcasted_iota(jnp.int32, (2 * tile, n * pad), 0)
    wanted = jnp.where(j_idx < tile, pair_ref[0, 0] * tile + j_idx, pair_ref[0, 1] * tile + j_idx - tile)
    select32 = (jnp.abs(places - 1.0 - wanted.astype(f32)) < 0.5).astype(f32)
    select = select32.astype(jnp.bfloat16)
    back = jnp.transpose(select32).astype(jnp.bfloat16)
    valid = lax.broadcasted_iota(jnp.int32, (n * pad, 2 * lanes), 0) % pad < rows

    relay(0)
    loads[0].wait()
    steps = tile // block
    span = block * tile
    for c in range(chunks):
        if c + 1 < chunks:
            relay(c + 1)
        forward(c, 1 - core).wait_recv()
        whole = jnp.where(valid, gath[c].reshape(n * pad, 2 * lanes), 0.0)
        high, rest = split(whole)
        low = (whole - high.astype(f32) - rest.astype(f32)).astype(jnp.bfloat16)
        fetched[c] = mm(select, high) + mm(select, rest) + mm(select, low)

        @pl.loop(0, steps, unroll=True)
        def _(b):
            p0 = pl.multiple_of(b * block, block)
            at = pl.ds(pl.multiple_of(b * span, span), span)
            left = fetched[c, pl.ds(p0, block), :]
            lre, lim = left[:, None, :lanes], left[:, None, lanes:]
            right = fetched[c, pl.ds(tile, tile), :]
            rre, rim = right[None, :, :lanes], right[None, :, lanes:]
            real = (lre * rre + lim * rim).reshape(span, lanes)
            imag = (lim * rre - lre * rim).reshape(span, lanes)
            high, low = split(jnp.concatenate([real, imag], -1))
            got = mm(high, down[0, c]) + mm(low, down[0, c]) + mm(high, down[1, c])
            if c > 0:
                got = got + lag[at, :]
            if c < chunks - 1:
                lag[at, :] = got
            else:
                misfit = got - seen[at, :]
                weighted = misfit + cubic_weight * misfit * misfit * misfit
                high, low = split(weighted)
                whigh[at, :] = high
                wlow[at, :] = low

        if c == chunks - 2:
            loads[1].wait()
    loads[2].wait()

    def swap(c):
        return remote(
            sendbuf.at[c, 1 - core, :, real_rows, :], halfbuf.at[c, :, real_rows, :],
            s1send.at[c], s1recv.at[c], mine, 1 - core,
        )

    def deliver(c, k):
        return remote(
            sumbuf.at[c, other(k), real_rows, :], recvbuf.at[c, k, real_rows, :],
            s2send.at[c, k], s2recv.at[c, k], other(k), core,
        )

    def combine(c):
        swap(c).wait_recv()
        sumbuf[c] = sendbuf[c, core] + halfbuf[c]

        @pl.loop(1, pairs)
        def _(k):
            deliver(c, k).start()

    for c in range(chunks):
        acc[pl.ds(tile, tile), :] = jnp.zeros((tile, 2 * lanes), f32)

        @pl.loop(0, steps, unroll=True)
        def _(b):
            p0 = pl.multiple_of(b * block, block)
            at = pl.ds(pl.multiple_of(b * span, span), span)
            high, low = whigh[at, :], wlow[at, :]
            got = mm(high, up[0, c]) + mm(low, up[0, c]) + mm(high, up[1, c])
            got = got.reshape(block, tile, 2 * lanes)
            are, aim = got[:, :, :lanes], got[:, :, lanes:]
            left = fetched[c, pl.ds(p0, block), :]
            lre, lim = left[:, None, :lanes], left[:, None, lanes:]
            right = fetched[c, pl.ds(tile, tile), :]
            rre, rim = right[None, :, :lanes], right[None, :, lanes:]
            acc[pl.ds(p0, block), pl.ds(0, lanes)] = jnp.sum(are * rre - aim * rim, 1)
            acc[pl.ds(p0, block), pl.ds(lanes, lanes)] = jnp.sum(are * rim + aim * rre, 1)
            acc[pl.ds(tile, tile), pl.ds(0, lanes)] += jnp.sum(are * lre + aim * lim, 0)
            acc[pl.ds(tile, tile), pl.ds(lanes, lanes)] += jnp.sum(are * lim - aim * lre, 0)

        high, low = split(acc[...])
        sendbuf[c] = (mm(back, high) + mm(back, low)).reshape(2, pairs, pad, 2 * lanes)
        swap(c).start()
        if c > 0:
            combine(c - 1)
    combine(chunks - 1)

    for c in range(chunks):
        @pl.loop(1, pairs)
        def _(k):
            deliver(c, k).wait_recv()

        total = sumbuf[c, mine]
        for k in range(1, pairs):
            total = total + recvbuf[c, k]
        total = total * (1.0 / tile)
        for h in range(2):
            out_ref[:, h * chunks + c, :] = total[:rows, h * lanes:(h + 1) * lanes]

    for c in range(chunks):
        forward(c, core).wait_send()
        swap(c).wait_send()

        @pl.loop(1, pairs)
        def _(k):
            spread(c, k, mine).wait_send()
            deliver(c, k).wait_send()


def one_kernel(mesh, spectra, station_place, tiles, observed):
    n_sta, n_band = mesh.shape["sta"], mesh.shape["band"]
    n = n_sta * n_band
    tile, lags = observed.shape[1], observed.shape[3]
    rows, width = spectra.shape[1], spectra.shape[2]
    lanes = LANES
    half = width // 2
    chunks = half // lanes
    pad = -(-rows // 8) * 8
    block = 8
    down, up = tables(half, lags, lanes)
    f32, bf16 = jnp.float32, jnp.bfloat16
    dma = pltpu.SemaphoreType.DMA
    anywhere = pl.BlockSpec(memory_space=pl.ANY)
    out = pl.pallas_call(
        functools.partial(fused, (n_sta, n_band), (tile, rows, pad, lanes, chunks, block)),
        out_shape=jax.ShapeDtypeStruct((rows, 2 * chunks, lanes), f32),
        in_specs=[
            pl.BlockSpec(memory_space=pltpu.SMEM), pl.BlockSpec(memory_space=pltpu.VMEM),
            anywhere, anywhere, anywhere, anywhere,
        ],
        out_specs=pl.BlockSpec(memory_space=pltpu.VMEM),
        scratch_shapes=[
            pltpu.VMEM((chunks, 2, n // 2, pad, 2 * lanes), f32),
            pltpu.VMEM((tile * tile, lags), f32),
            pltpu.VMEM(down.shape, bf16),
            pltpu.VMEM(up.shape, bf16),
            pltpu.VMEM((tile * tile, lags), f32),
            pltpu.VMEM((tile * tile, lags), bf16),
            pltpu.VMEM((tile * tile, lags), bf16),
            pltpu.VMEM((chunks, 2 * tile, 2 * lanes), f32),
            pltpu.VMEM((2 * tile, 2 * lanes), f32),
            pltpu.VMEM((chunks, 2, n // 2, pad, 2 * lanes), f32),
            pltpu.VMEM((chunks, n // 2, pad, 2 * lanes), f32),
            pltpu.VMEM((chunks, n // 2, pad, 2 * lanes), f32),
            pltpu.VMEM((chunks, n // 2, pad, 2 * lanes), f32),
            dma((rows, 2)), dma((3,)),
            dma((chunks, n // 2)), dma((chunks, n // 2)), dma((chunks,)), dma((chunks,)),
            dma((chunks,)), dma((chunks,)), dma((chunks, n // 2)), dma((chunks, n // 2)),
        ],
        compiler_params=pltpu.CompilerParams(collective_id=0, has_side_effects=True),
        name="adjoint_kernel",
    )(
        tiles, station_place.reshape(1, -1), spectra.reshape(rows, 2 * chunks, lanes),
        observed.reshape(tile * tile, lags), jnp.asarray(down), jnp.asarray(up),
    )
    return out.reshape(1, rows, width)


def solution(mesh):
    placed = (
        P("src", ("grp", "sta", "band"), None),
        P("grp"),
        P(("grp", "sta", "band"), None),
        P(("grp", "sta", "band"), None, None, None),
    )
    def body(spectra, station_place, tiles, observed):
        fits = (
            mesh.shape["src"] == 1 and mesh.shape["band"] % 2 == 0 and spectra.shape[0] == 1 and tiles.shape[0] == 1
            and spectra.shape[2] % (2 * LANES) == 0 and observed.shape[1] % 8 == 0
        )
        if fits:
            return one_kernel(mesh, spectra, station_place, tiles, observed)
        return local(spectra, station_place, tiles, observed)

    return jax.shard_map(
        body,
        mesh=mesh,
        in_specs=placed,
        out_specs=P("src", ("grp", "sta", "band"), None),
        check_vma=False,
    )
```
